32 devices in a mesh: batch: 4 (over y, x), ctx: 8 (over z, core).
Axes of the slice: x: 2, y: 2, z: 4, core: 2. Of those that a mesh axis runs over, the one named last changes fastest.
Arguments:
- hidden: bfloat16 [4, 1024, 768], P('batch', 'ctx'), may hold values from -6 to 6
- cotangent: bfloat16 [4, 1024, 768], P('batch', 'ctx'), may hold values from -6 to 6
- w_qkv: bfloat16 [768, 2304], P(('batch', 'ctx')), may hold values from -3 to 3
- w_proj: bfloat16 [768, 768], P(('batch', 'ctx')), may hold values from -1.25 to 1.25
- w_inner: bfloat16 [768, 2304], P(('batch', 'ctx')), may hold values from -0.21875 to 0.21875
- w_down: bfloat16 [768, 1152], P(('batch', 'ctx')), may hold values from -0.1875 to 0.1875
- norm1_gain: bfloat16 [768], P(('batch', 'ctx')), may hold values from 0.5 to 1.5
- norm2_gain: bfloat16 [768], P(('batch', 'ctx')), may hold values from 0.5 to 1.5
Outputs:
- hidden_out: bfloat16 [4, 1024, 768], P('batch', 'ctx')
- hidden_grad: float32 [4, 1024, 768], P('batch', 'ctx')
- qkv_grad: float32 [768, 2304], P(('batch', 'ctx'))
- proj_grad: float32 [768, 768], P(('batch', 'ctx'))
- inner_grad: float32 [768, 2304], P(('batch', 'ctx'))
- down_grad: float32 [768, 1152], P(('batch', 'ctx'))
- norm1_grad: float32 [768], P(('batch', 'ctx'))
- norm2_grad: float32 [768], P(('batch', 'ctx'))
The draws below stay inside these ranges and needn't reach their ends.
All inputs are finite; a program needn't handle non-finite values.
Results may differ from the reference program's by a relative error of at most 0.02.
Values may be sent and summed in bfloat16 or wider, within the bound.
A program may use at most 192 MiB of HBM per device.

```python
import jax
import jax.numpy as jnp
from jax import lax

D = 768
HEADS = 12
HEAD_DIM = 64
FF = 1152
LEN = 1024
SEQS = 4


def draw_w_qkv(key, part):
    spread_scale = (D // 2) ** (-0.5)
    sample = jnp.clip(jax.random.normal(key, (D, 3 * D), jnp.float32), -6.0, 6.0)
    return (sample * spread_scale).astype(jnp.bfloat16)


def with_spikes(drawn, own_key, source, target, blocks, factor):
    def block_of(dim):
        return (jnp.arange(drawn.shape[dim]) // (drawn.shape[dim] // blocks)).reshape((-1,) + (1,) * (drawn.ndim - 1 - dim))

    one_side = jax.random.permutation(own_key, blocks)[block_of(target)]
    far = (block_of(target) + blocks // 2) % blocks
    return jnp.where((block_of(source) == one_side) | (block_of(source) == far), factor * drawn, drawn)


def level_of(stream_key, dims, shards, low, high):
    def one(dim, blocks):
        heights = jax.random.uniform(jax.random.fold_in(jax.random.fold_in(stream_key, 6), dim), (blocks,), jnp.float32, low / len(shards), high / len(shards))
        return jnp.repeat(jnp.exp(heights), dims[dim] // blocks).reshape((-1,) + (1,) * (len(dims) - dim - 1))

    loudness = one(*shards[0])
    for cut in shards[1:]:
        loudness = loudness * one(*cut)
    return loudness


def gaussian(own_key, shape, width, most, cuts=(), kind=jnp.bfloat16):
    drawn = width * jax.random.normal(own_key, shape, jnp.float32)
    if cuts:
        drawn = drawn * level_of(own_key, shape, cuts, -0.22, 0.18)
    return jnp.clip(drawn, -most, most).astype(kind)


def noise_with(key, shape, scale, most, pieces, heavy, kind=jnp.bfloat16):
    array = scale * jax.random.normal(key, shape, jnp.float32)
    if pieces:
        array = array * level_of(key, shape, pieces, -0.22, 0.18)
    return jnp.clip(with_spikes(array, jax.random.fold_in(key, 3), *heavy), -most, most).astype(kind)


def setup_inputs(seed: int = 0) -> dict:
    arg_keys = jax.random.split(jax.random.key(seed), 9)
    return {
        "hidden": gaussian(arg_keys[0], (SEQS, LEN, D), 1.0, 6.0, ((0, 4), (1, 8))),
        "cotangent": noise_with(arg_keys[1], (SEQS, LEN, D), 1.0, 6.0, ((0, 4), (1, 8)), (1, 2, 8, 2.0)),
        "w_qkv": draw_w_qkv(jax.random.fold_in(arg_keys[8], 71), 0),
        "w_proj": gaussian(arg_keys[3], (D, D), (D // 32) ** -0.5, 1.25, ((0, 32),)),
        "w_inner": gaussian(arg_keys[4], (D, 2 * FF), D ** -0.5, 0.21875, ((0, 32),)),
        "w_down": gaussian(arg_keys[5], (D, FF), FF ** -0.5, 0.1875, ((0, 32),)),
        "norm1_gain": jnp.clip(1.0 + 0.1 * jax.random.normal(arg_keys[6], (D,), jnp.float32), 0.5, 1.5).astype(jnp.bfloat16),
        "norm2_gain": jnp.clip(1.0 + 0.1 * jax.random.normal(arg_keys[7], (D,), jnp.float32), 0.5, 1.5).astype(jnp.bfloat16),
    }


norm_eps = 1e-05
rope_base = 160000.0

def apply_layer_norm(values, gain_vector):
    centre = lax.optimization_barrier(jnp.mean(values, axis=-1, keepdims=True))
    shifted = values - centre
    spread = lax.optimization_barrier(jnp.mean(shifted * shifted, axis=-1, keepdims=True))
    inverse = lax.rsqrt(spread + norm_eps)
    normed = shifted * inverse
    return (normed * gain_vector, normed, inverse)

def layer_norm_gradient(upstream, gain_vector, normed, inverse):
    scaled = upstream * gain_vector
    first_mean = lax.optimization_barrier(jnp.mean(scaled, axis=-1, keepdims=True))
    second_mean = lax.optimization_barrier(jnp.mean(scaled * normed, axis=-1, keepdims=True))
    return (inverse * (scaled - first_mean - normed * second_mean), lax.optimization_barrier(jnp.sum(upstream * normed, axis=0)))

def rope_tables(offset, row_count, head_width):
    half_dim = head_width // 2
    position = (offset + jnp.arange(row_count, dtype=jnp.int32)).astype(jnp.float32)
    exponent = jnp.arange(half_dim, dtype=jnp.int32).astype(jnp.float32) * (-2.0 / head_width)
    angles = position[:, None] * jnp.power(rope_base, exponent)[None, :]
    return (jnp.cos(angles), jnp.sin(angles))

def rotate(values, cosine, sine_table, direction):
    half_dim = values.shape[-1] // 2
    front_half = values[..., :half_dim]
    back_half = values[..., half_dim:]
    cos_rows = cosine[:, None, :]
    sin_rows = sine_table[:, None, :] * direction
    return jnp.concatenate([front_half * cos_rows - back_half * sin_rows, back_half * cos_rows + front_half * sin_rows], axis=-1)

def gelu_parts(act_input):
    normal_cdf = 0.5 * (1.0 + jax.scipy.special.erf(act_input * 0.7071067811865476))
    density = jnp.exp(-0.5 * act_input * act_input) * 0.3989422804014327
    return (act_input * normal_cdf, normal_cdf + act_input * density)

def rounded(values):
    return lax.optimization_barrier(values.astype(jnp.bfloat16)).astype(jnp.float32)

def reference(hidden, cotangent, w_qkv, w_proj, w_inner, w_down, norm1_gain, norm2_gain):
    seq_length = hidden.shape[1]
    block_rows = min(512, seq_length)
    block_count = seq_length // block_rows
    score_scale = HEAD_DIM ** (-0.5)
    highest = lax.Precision.HIGHEST
    first_norm_gain = norm1_gain.astype(jnp.float32)
    second_norm_gain = norm2_gain.astype(jnp.float32)
    cosine, sine_table = rope_tables(0, seq_length, HEAD_DIM)

    def one_sequence(grad_totals, sequence_pair):
        token_rows, upstream = sequence_pair
        input_tokens = token_rows.astype(jnp.float32)
        first_normed_rows, first_centered_rows, first_inverse_deviation = apply_layer_norm(input_tokens, first_norm_gain)
        h_one = first_normed_rows.astype(jnp.bfloat16)
        projected = jnp.dot(h_one, w_qkv, preferred_element_type=jnp.float32)
        query_rot = rotate(projected[:, :D].reshape(seq_length, HEADS, HEAD_DIM), cosine, sine_table, 1.0).astype(jnp.bfloat16)
        key_rot = rotate(projected[:, D:2 * D].reshape(seq_length, HEADS, HEAD_DIM), cosine, sine_table, 1.0).astype(jnp.bfloat16)
        value_rows = projected[:, 2 * D:].reshape(seq_length, HEADS, HEAD_DIM).astype(jnp.bfloat16)
        key_wide = key_rot.astype(jnp.float32)
        value_wide = value_rows.astype(jnp.float32)

        def attend(query_block):
            scores = jnp.einsum('qhd,khd->hqk', query_block.astype(jnp.float32), key_wide) * score_scale
            row_peak = lax.optimization_barrier(jnp.max(scores, axis=-1))
            log_total = row_peak + jnp.log(lax.optimization_barrier(jnp.sum(jnp.exp(scores - row_peak[..., None]), axis=-1)))
            weights_low = rounded(jnp.exp(scores - log_total[..., None]))
            mixture = jnp.einsum('hqk,khd->qhd', weights_low, value_wide, precision=highest)
            return (mixture, log_total)
        mixture, log_totals = lax.map(attend, query_rot.reshape(block_count, block_rows, HEADS, HEAD_DIM))
        attended = mixture.reshape(seq_length, D).astype(jnp.bfloat16)
        residual_stream = input_tokens + jnp.dot(attended, w_proj, preferred_element_type=jnp.float32)
        second_normed_rows, second_centered_rows, second_inverse_deviation = apply_layer_norm(residual_stream, second_norm_gain)
        h_two = second_normed_rows.astype(jnp.bfloat16)
        inner_all = jnp.dot(h_two, w_inner, preferred_element_type=jnp.float32)
        act_half = inner_all[:, :FF]
        gate_half = inner_all[:, FF:]
        activated, gelu_slope = gelu_parts(act_half)
        middle = (activated * gate_half).astype(jnp.bfloat16)
        output_rows = residual_stream + jnp.dot(middle, w_down.T, preferred_element_type=jnp.float32)
        d_middle = jnp.dot(upstream, w_down, preferred_element_type=jnp.float32)
        down_part = jnp.dot(upstream.T, middle, preferred_element_type=jnp.float32)
        d_inner = jnp.concatenate([d_middle * gate_half * gelu_slope, d_middle * activated], axis=-1).astype(jnp.bfloat16)
        inner_part = jnp.dot(h_two.T, d_inner, preferred_element_type=jnp.float32)
        second_hidden_gradient = jnp.dot(d_inner, w_inner.T, preferred_element_type=jnp.float32)
        residual_norm_gradient, second_gain_portion = layer_norm_gradient(second_hidden_gradient, second_norm_gain, second_centered_rows, second_inverse_deviation)
        d_resid = upstream.astype(jnp.float32) + residual_norm_gradient
        d_resid_low = d_resid.astype(jnp.bfloat16)
        proj_part = jnp.dot(attended.T, d_resid_low, preferred_element_type=jnp.float32)
        d_attended = jnp.dot(d_resid_low, w_proj.T, preferred_element_type=jnp.float32).astype(jnp.bfloat16)
        grad_heads = d_attended.reshape(seq_length, HEADS, HEAD_DIM)
        row_delta = lax.optimization_barrier(jnp.sum(grad_heads.astype(jnp.float32) * attended.reshape(seq_length, HEADS, HEAD_DIM).astype(jnp.float32), axis=-1))
        delta_blocks = jnp.transpose(row_delta.reshape(block_count, block_rows, HEADS), (0, 2, 1))

        def attend_back(running, block_items):
            query_block, grad_block, log_block, delta_block = block_items
            query_wide = query_block.astype(jnp.float32)
            grad_wide = grad_block.astype(jnp.float32)
            scores = jnp.einsum('qhd,khd->hqk', query_wide, key_wide) * score_scale
            probabilities = jnp.exp(scores - log_block[..., None])
            probs_low = rounded(probabilities)
            grad_dots = jnp.einsum('qhd,khd->hqk', grad_wide, value_wide)
            dscore = rounded(probabilities * (grad_dots - delta_block[..., None]))
            query_grad = jnp.einsum('hqk,khd->qhd', dscore, key_wide) * score_scale
            key_sum = running[0] + jnp.einsum('hqk,qhd->khd', dscore, query_wide) * score_scale
            value_sum = running[1] + jnp.einsum('hqk,qhd->khd', probs_low, grad_wide)
            return ((key_sum, value_sum), query_grad)
        zero_heads = jnp.zeros((seq_length, HEADS, HEAD_DIM), jnp.float32)
        (key_grad, value_grad), query_grad = lax.scan(attend_back, (zero_heads, zero_heads), (query_rot.reshape(block_count, block_rows, HEADS, HEAD_DIM), grad_heads.reshape(block_count, block_rows, HEADS, HEAD_DIM), log_totals, delta_blocks))
        query_grad = query_grad.reshape(seq_length, HEADS, HEAD_DIM)
        d_query = rotate(query_grad, cosine, sine_table, -1.0)
        d_key = rotate(key_grad, cosine, sine_table, -1.0)
        d_projected = jnp.concatenate([d_query.reshape(seq_length, D), d_key.reshape(seq_length, D), value_grad.reshape(seq_length, D)], axis=-1).astype(jnp.bfloat16)
        qkv_part = jnp.dot(h_one.T, d_projected, preferred_element_type=jnp.float32)
        first_hidden_gradient = jnp.dot(d_projected, w_qkv.T, preferred_element_type=jnp.float32)
        input_norm_gradient, first_gain_portion = layer_norm_gradient(first_hidden_gradient, first_norm_gain, first_centered_rows, first_inverse_deviation)
        input_grad = d_resid + input_norm_gradient
        new_totals = (grad_totals[0] + qkv_part, grad_totals[1] + proj_part, grad_totals[2] + inner_part, grad_totals[3] + down_part, grad_totals[4] + first_gain_portion, grad_totals[5] + second_gain_portion)
        return (new_totals, (output_rows.astype(jnp.bfloat16), input_grad))
    start_totals = (jnp.zeros((D, 3 * D), jnp.float32), jnp.zeros((D, D), jnp.float32), jnp.zeros((D, 2 * FF), jnp.float32), jnp.zeros((D, FF), jnp.float32), jnp.zeros((D,), jnp.float32), jnp.zeros((D,), jnp.float32))
    grad_totals, (hidden_out, hidden_grad) = lax.scan(one_sequence, start_totals, (hidden, cotangent))
    return (hidden_out, hidden_grad, grad_totals[0], grad_totals[1], grad_totals[2], grad_totals[3], grad_totals[4], grad_totals[5])
```

```python
import functools
import math

import jax
import jax.numpy as jnp
from jax import lax
from jax.experimental import pallas as pl
from jax.experimental.pallas import tpu as pltpu
from jax.sharding import PartitionSpec as P

D = 768
HEADS = 12
HEAD_DIM = 64
FF = 1152


norm_eps = 1e-05
rope_base = 160000.0


def apply_layer_norm(values, gain_vector):
    centre = jnp.mean(values, axis=-1, keepdims=True)
    shifted = values - centre
    spread = jnp.mean(shifted * shifted, axis=-1, keepdims=True)
    inverse = lax.rsqrt(spread + norm_eps)
    normed = shifted * inverse
    return (normed * gain_vector, normed, inverse)


def layer_norm_gradient(upstream, gain_vector, normed, inverse):
    scaled = upstream * gain_vector
    first_mean = jnp.mean(scaled, axis=-1, keepdims=True)
    second_mean = jnp.mean(scaled * normed, axis=-1, keepdims=True)
    return (
        inverse * (scaled - first_mean - normed * second_mean),
        jnp.sum(upstream * normed, axis=0),
    )


def rope_tables(offset, row_count, head_width):
    half_dim = head_width // 2
    position = (offset + jnp.arange(row_count, dtype=jnp.int32)).astype(jnp.float32)
    exponent = jnp.arange(half_dim, dtype=jnp.int32).astype(jnp.float32) * (-2.0 / head_width)
    angles = position[:, None] * jnp.power(rope_base, exponent)[None, :]
    return (jnp.cos(angles), jnp.sin(angles))


def rotate(values, cosine, sine_table, direction):
    half_dim = values.shape[-1] // 2
    front_half = values[..., :half_dim]
    back_half = values[..., half_dim:]
    cos_rows = cosine[:, None, :]
    sin_rows = sine_table[:, None, :] * direction
    return jnp.concatenate(
        [
            front_half * cos_rows - back_half * sin_rows,
            back_half * cos_rows + front_half * sin_rows,
        ],
        axis=-1,
    )


def gelu_parts(act_input):
    normal_cdf = 0.5 * (1.0 + jax.scipy.special.erf(act_input * 0.7071067811865476))
    density = jnp.exp(-0.5 * act_input * act_input) * 0.3989422804014327
    return (act_input * normal_cdf, normal_cdf + act_input * density)


def as_heads(flat_rows):
    return flat_rows.reshape(flat_rows.shape[0], HEADS, HEAD_DIM)


EVERY = ("batch", "ctx")
LANES = 128


def weight_grad_kernel(bounds, *refs):
    count = len(bounds) - 1
    lefts, rights, gains_ref, out_ref = refs[:count], refs[count : 2 * count], refs[-2], refs[-1]
    step = pl.program_id(0)
    for index in range(count):

        @pl.when(jnp.logical_and(step >= bounds[index], step < bounds[index + 1]))
        def _(left=lefts[index], right=rights[index]):
            out_ref[...] = lax.dot_general(
                left[...],
                right[...],
                (((0,), (0,)), ((), ())),
                preferred_element_type=jnp.float32,
            ).astype(out_ref.dtype)

    @pl.when(step == bounds[count])
    def _():
        out_ref[:, :LANES] = gains_ref[...].astype(out_ref.dtype)


def weight_grads(pairs, gain_columns):
    rows, width = pairs[0][0].shape
    widths = [right.shape[1] for _, right in pairs]
    block = math.gcd(*widths)
    bounds = [0]
    for part in widths:
        bounds.append(bounds[-1] + part // block)

    def right_index(start, count, step):
        return (0, jnp.clip(step - start, 0, count - 1))

    whole = lambda step: (0, 0)
    total = sum(widths) + LANES
    return pl.pallas_call(
        functools.partial(weight_grad_kernel, tuple(bounds)),
        out_shape=jax.ShapeDtypeStruct((width, total), jnp.bfloat16),
        grid=(bounds[-1] + 1,),
        in_specs=[pl.BlockSpec((rows, width), whole) for _ in pairs]
        + [
            pl.BlockSpec(
                (rows, block),
                functools.partial(right_index, bounds[i], bounds[i + 1] - bounds[i]),
            )
            for i in range(len(pairs))
        ]
        + [pl.BlockSpec((width, LANES), whole)],
        out_specs=pl.BlockSpec((width, block), lambda step: (0, step)),
        cost_estimate=pl.CostEstimate(
            flops=2 * rows * width * total, bytes_accessed=2 * width * total, transcendentals=0
        ),
    )(*[left for left, _ in pairs], *[right for _, right in pairs], gain_columns)


def local(hidden, cotangent, w_qkv, w_proj, w_inner, w_down, norm1_gain, norm2_gain):
    token_rows = hidden.shape[1]
    score_scale = HEAD_DIM ** (-0.5)
    gains = jnp.pad(jnp.stack([norm1_gain, norm2_gain], axis=1), ((0, 0), (0, LANES - 2)))
    packed = lax.all_gather(
        jnp.concatenate([w_qkv, w_proj, w_inner, w_down, gains], axis=1), EVERY, axis=0, tiled=True
    )
    edges = [0]
    for part in (w_qkv, w_proj, w_inner, w_down, gains):
        edges.append(edges[-1] + part.shape[1])
    full_qkv, full_proj, full_inner, full_down, full_gains = (
        packed[:, edges[i] : edges[i + 1]] for i in range(5)
    )
    first_norm_gain = full_gains[:, 0].astype(jnp.float32)
    second_norm_gain = full_gains[:, 1].astype(jnp.float32)
    input_tokens = hidden[0].astype(jnp.float32)
    first_normed_rows, first_centered_rows, first_inverse_deviation = apply_layer_norm(
        input_tokens, first_norm_gain
    )
    h_one = first_normed_rows.astype(jnp.bfloat16)
    projected = jnp.dot(h_one, full_qkv, preferred_element_type=jnp.float32)
    cosine, sine_table = rope_tables(lax.axis_index("ctx") * token_rows, token_rows, HEAD_DIM)
    query_rot = rotate(as_heads(projected[:, :D]), cosine, sine_table, 1.0).astype(jnp.bfloat16)
    key_flat = (
        rotate(as_heads(projected[:, D : 2 * D]), cosine, sine_table, 1.0)
        .astype(jnp.bfloat16)
        .reshape(token_rows, D)
    )
    value_flat = projected[:, 2 * D :].astype(jnp.bfloat16)
    key_value = lax.all_gather(
        jnp.concatenate([key_flat, value_flat], axis=1), "ctx", axis=0, tiled=True
    )
    key_whole = as_heads(key_value[:, :D])
    value_whole = as_heads(key_value[:, D:])
    scores = (
        jnp.einsum("qhd,khd->hqk", query_rot, key_whole, preferred_element_type=jnp.float32)
        * score_scale
    )
    row_peak = jnp.max(scores, axis=-1)
    weights = jnp.exp(scores - row_peak[..., None])
    row_total = jnp.sum(weights, axis=-1)
    mixture = jnp.einsum(
        "hqk,khd->qhd",
        weights.astype(jnp.bfloat16),
        value_whole,
        preferred_element_type=jnp.float32,
    )
    attended = (
        (mixture / jnp.transpose(row_total)[:, :, None])
        .reshape(token_rows, D)
        .astype(jnp.bfloat16)
    )
    residual_stream = input_tokens + jnp.dot(
        attended, full_proj, preferred_element_type=jnp.float32
    )
    second_normed_rows, second_centered_rows, second_inverse_deviation = apply_layer_norm(
        residual_stream, second_norm_gain
    )
    h_two = second_normed_rows.astype(jnp.bfloat16)
    inner_all = jnp.dot(h_two, full_inner, preferred_element_type=jnp.float32)
    act_half = inner_all[:, :FF]
    gate_half = inner_all[:, FF:]
    activated, gelu_slope = gelu_parts(act_half)
    middle = (activated * gate_half).astype(jnp.bfloat16)
    output_rows = residual_stream + jnp.einsum(
        "tf,df->td", middle, full_down, preferred_element_type=jnp.float32
    )
    upstream = cotangent[0]
    d_middle = jnp.dot(upstream, full_down, preferred_element_type=jnp.float32)
    d_inner = jnp.concatenate(
        [d_middle * gate_half * gelu_slope, d_middle * activated], axis=-1
    ).astype(jnp.bfloat16)
    second_hidden_gradient = jnp.einsum(
        "te,de->td", d_inner, full_inner, preferred_element_type=jnp.float32
    )
    residual_norm_gradient, second_gain_portion = layer_norm_gradient(
        second_hidden_gradient, second_norm_gain, second_centered_rows, second_inverse_deviation
    )
    d_resid = upstream.astype(jnp.float32) + residual_norm_gradient
    d_resid_low = d_resid.astype(jnp.bfloat16)
    d_attended = jnp.einsum(
        "td,ed->te", d_resid_low, full_proj, preferred_element_type=jnp.float32
    ).astype(jnp.bfloat16)
    grad_heads = as_heads(d_attended)
    row_delta = jnp.transpose(
        jnp.sum(grad_heads.astype(jnp.float32) * as_heads(attended).astype(jnp.float32), axis=-1)
    )
    probabilities = weights * (1.0 / row_total)[..., None]
    grad_dots = jnp.einsum(
        "qhd,khd->hqk", grad_heads, value_whole, preferred_element_type=jnp.float32
    )
    dscore = (probabilities * (grad_dots - row_delta[..., None])).astype(jnp.bfloat16)
    probs_low = probabilities.astype(jnp.bfloat16)
    key_terms = (
        jnp.einsum("hqk,qhd->khd", dscore, query_rot, preferred_element_type=jnp.float32)
        * score_scale
    )
    value_terms = jnp.einsum(
        "hqk,qhd->khd", probs_low, grad_heads, preferred_element_type=jnp.float32
    )
    whole_rows = key_value.shape[0]
    key_value_sum = lax.psum_scatter(
        jnp.concatenate(
            [
                key_terms.reshape(whole_rows, D).astype(jnp.bfloat16),
                value_terms.reshape(whole_rows, D).astype(jnp.bfloat16),
            ],
            axis=1,
        ),
        "ctx",
        scatter_dimension=0,
        tiled=True,
    )
    query_grad = (
        jnp.einsum("hqk,khd->qhd", dscore, key_whole, preferred_element_type=jnp.float32)
        * score_scale
    )
    d_query = rotate(query_grad, cosine, sine_table, -1.0)
    d_key = rotate(as_heads(key_value_sum[:, :D].astype(jnp.float32)), cosine, sine_table, -1.0)
    d_projected = jnp.concatenate(
        [
            d_query.reshape(token_rows, D).astype(jnp.bfloat16),
            d_key.reshape(token_rows, D).astype(jnp.bfloat16),
            key_value_sum[:, D:],
        ],
        axis=-1,
    )
    first_hidden_gradient = jnp.einsum(
        "te,de->td", d_projected, full_qkv, preferred_element_type=jnp.float32
    )
    input_norm_gradient, first_gain_portion = layer_norm_gradient(
        first_hidden_gradient, first_norm_gain, first_centered_rows, first_inverse_deviation
    )
    input_grad = d_resid + input_norm_gradient
    gain_columns = jnp.pad(
        jnp.stack([first_gain_portion, second_gain_portion], axis=1), ((0, 0), (0, LANES - 2))
    )
    grad_terms = weight_grads(
        [(h_one, d_projected), (attended, d_resid_low), (h_two, d_inner), (upstream, middle)],
        gain_columns,
    )
    grad_share = lax.psum_scatter(
        grad_terms, EVERY, scatter_dimension=0, tiled=True
    ).astype(jnp.float32)
    return (
        output_rows.astype(jnp.bfloat16)[None],
        input_grad[None],
        grad_share[:, edges[0] : edges[1]],
        grad_share[:, edges[1] : edges[2]],
        grad_share[:, edges[2] : edges[3]],
        grad_share[:, edges[3] : edges[4]],
        grad_share[:, edges[4]],
        grad_share[:, edges[4] + 1],
    )


MESH = pl.DeviceIdType.MESH
LANES = 128
TYPE = 256
F32 = jnp.float32
BF16 = jnp.bfloat16


def place():
    b = lax.axis_index("batch")
    t = lax.axis_index("ctx")
    return b, t // 2, t % 2


def plane_x(b):
    return b + 1 - 2 * (b % 2)


def plane_y(b):
    return b + 2 - 4 * (b // 2)


def remote(src, dst, send_sem, recv_sem, b, t):
    return pltpu.make_async_remote_copy(
        src_ref=src,
        dst_ref=dst,
        send_sem=send_sem,
        recv_sem=recv_sem,
        device_id=(b, t),
        device_id_type=MESH,
    )


def greet(partners):
    barrier = pltpu.get_barrier_semaphore()
    for b, t in partners:
        pl.semaphore_signal(barrier, inc=1, device_id=(b, t), device_id_type=MESH)
    pl.semaphore_wait(barrier, len(partners))


class Sends:
    def __init__(self, sems):
        self.sems, self.count, self.open = sems, 0, []

    def go(self, src, dst, recv_sem, b, t, cond=None):
        copy = remote(src, dst, self.sems.at[self.count], recv_sem, b, t)
        self.count += 1
        self.open.append((copy, cond))
        if cond is None:
            copy.start()
        else:
            pl.when(cond)(copy.start)

    def drain(self):
        for copy, cond in self.open:
            if cond is None:
                copy.wait_send()
            else:
                pl.when(cond)(copy.wait_send)
        self.open = []


def both(*conds):
    conds = [c for c in conds if c is not None]
    if not conds:
        return None
    out = conds[0]
    for c in conds[1:]:
        out = jnp.logical_and(out, c)
    return out


def front_kernel(
    depth,
    tokens,
    heads,
    hidden_ref,
    wq_ref,
    rest_ref,
    rest_all,
    att_ref,
    q_ref,
    k_ref,
    v_ref,
    o_ref,
    lse_ref,
    h1_ref,
    wq_out,
    gain_out,
    hid_all,
    wq_all,
    att_own,
    cos_ref,
    sin_ref,
    send_sems,
    hid_sems,
    wq_sems,
    rest_sems,
    half_sems,
    att_sems,
    own_sems,
):
    b, z, c = place()
    t = 2 * z + c
    bx, by = plane_x(b), plane_y(b)
    bd = plane_x(by)
    shard = lambda bb, zz, cc: (bb * depth + zz) * 2 + cc
    mine = shard(b, z, c)
    sib = (b, 2 * z + 1 - c)
    partners = [(b, 2 * ((z + k) % depth) + c) for k in range(1, depth)]
    partners += [(bx, t), (by, t), sib]
    greet(partners)
    sends = Sends(send_sems)
    left_ok, right_ok = z > 0, z < depth - 1
    left, right = (b, t - 2), (b, t + 2)

    def arrive(dst, sem, cond=None):
        copy = remote(dst, dst, send_sems.at[0], sem, *sib)
        if cond is None:
            copy.wait_recv()
        else:
            pl.when(cond)(copy.wait_recv)

    def hid(slot):
        return hid_all.at[slot]

    def hid_start():
        for dst, cond in ((left, left_ok), (right, right_ok), (sib, None)):
            sends.go(hidden_ref, hid(t), hid_sems.at[t], *dst, cond=cond)
        pltpu.make_async_copy(hidden_ref, hid(t), own_sems.at[0]).start()

    def hid_step(k):
        lo, hi = z >= k, z < depth - k
        src = t - 2 * k
        src_lo = jnp.maximum(src, 0)
        arrive(hid(src_lo), hid_sems.at[src_lo], lo)
        if k < depth - 1:
            sends.go(hid(src_lo), hid(src_lo), hid_sems.at[src_lo], *right, cond=both(lo, right_ok))
        sends.go(hid(src_lo), hid(src_lo), hid_sems.at[src_lo], *sib, cond=lo)
        src_hi = jnp.minimum(t + 2 * k, 2 * depth - 1)
        arrive(hid(src_hi), hid_sems.at[src_hi], hi)
        if k < depth - 1:
            sends.go(hid(src_hi), hid(src_hi), hid_sems.at[src_hi], *left, cond=both(hi, left_ok))
        sends.go(hid(src_hi), hid(src_hi), hid_sems.at[src_hi], *sib, cond=hi)

    def wq_start():
        for k in range(1, depth):
            zz = (z + k) % depth
            sends.go(wq_ref.at[zz], wq_all.at[mine], wq_sems.at[mine], b, 2 * zz + c)
        pltpu.make_async_copy(wq_ref.at[z], wq_all.at[mine], own_sems.at[1]).start()
        for dst in ((bx, t), (by, t), sib):
            sends.go(wq_ref.at[z], wq_all.at[mine], wq_sems.at[mine], *dst)

    def wq_pass(i, targets):
        for dst in targets:
            sends.go(wq_all.at[i], wq_all.at[i], wq_sems.at[i], *dst)

    def wq_z():
        for k in range(1, depth):
            i = shard(b, (z + k) % depth, c)
            arrive(wq_all.at[i], wq_sems.at[i])
            wq_pass(i, ((bx, t), (by, t), sib))

    def wq_plane():
        for k in range(depth):
            zz = (z + k) % depth
            low = zz < depth // 2
            i = shard(bx, zz, c)
            arrive(wq_all.at[i], wq_sems.at[i])
            sends.go(wq_all.at[i], wq_all.at[i], wq_sems.at[i], by, t, cond=low)
            wq_pass(i, (sib,))
            i = shard(by, zz, c)
            arrive(wq_all.at[i], wq_sems.at[i])
            sends.go(
                wq_all.at[i], wq_all.at[i], wq_sems.at[i], bx, t, cond=jnp.logical_not(low)
            )
            wq_pass(i, (sib,))

    def wq_diag():
        for k in range(depth):
            i = shard(bd, (z + k) % depth, c)
            arrive(wq_all.at[i], wq_sems.at[i])
            wq_pass(i, (sib,))

    def wq_sib():
        for bb in range(4):
            for zz in range(depth):
                i = shard(bb, zz, 1 - c)
                arrive(wq_all.at[i], wq_sems.at[i])

    width = rest_ref.shape[1]
    cut = width // 2 // LANES * LANES
    part_a, part_b = pl.ds(0, cut), pl.ds(cut, width - cut)

    def rest(i):
        return rest_all.at[i]

    def rest_start():
        for dst, cond in (((bx, t), None), ((by, t), None), (left, left_ok), (right, right_ok), (sib, None)):
            sends.go(rest_ref, rest(mine), rest_sems.at[mine], *dst, cond=cond)
        pltpu.make_async_copy(rest_ref, rest(mine), own_sems.at[2]).start()

    def rest_z(k, side):
        cond = (z >= k) if side < 0 else (z < depth - k)
        zz = jnp.clip(z + side * k, 0, depth - 1)
        onward, on_ok = (right, right_ok) if side < 0 else (left, left_ok)
        i = shard(b, zz, c)
        arrive(rest(i), rest_sems.at[i], cond)
        if k < depth - 1:
            sends.go(rest(i), rest(i), rest_sems.at[i], *onward, cond=both(cond, on_ok))
        for dst in ((bx, t), (by, t), sib):
            sends.go(rest(i), rest(i), rest_sems.at[i], *dst, cond=cond)

    def slot(k, side):
        cond = None if k == 0 else ((z >= k) if side < 0 else (z < depth - k))
        return cond, (z if k == 0 else jnp.clip(z + side * k, 0, depth - 1))

    def rest_plane(k, side):
        cond, zz = slot(k, side)
        i = shard(bx, zz, c)
        arrive(rest(i), rest_sems.at[i], cond)
        sends.go(rest(i).at[:, part_a], rest(i).at[:, part_a], half_sems.at[0, i], by, t, cond=cond)
        sends.go(rest(i), rest(i), rest_sems.at[i], *sib, cond=cond)
        i = shard(by, zz, c)
        arrive(rest(i), rest_sems.at[i], cond)
        sends.go(rest(i).at[:, part_b], rest(i).at[:, part_b], half_sems.at[1, i], bx, t, cond=cond)
        sends.go(rest(i), rest(i), rest_sems.at[i], *sib, cond=cond)

    def rest_diag(k, side):
        cond, zz = slot(k, side)
        i = shard(bd, zz, c)
        arrive(rest(i).at[:, part_a], half_sems.at[0, i], cond)
        arrive(rest(i).at[:, part_b], half_sems.at[1, i], cond)
        sends.go(rest(i), rest(i), rest_sems.at[i], *sib, cond=cond)

    def rest_sib():
        for bb in range(4):
            for zz in range(depth):
                i = shard(bb, zz, 1 - c)
                arrive(rest(i), rest_sems.at[i])

    order = [(0, 0)] + [(k, s) for k in range(1, depth) for s in (-1, 1)]
    steps = []
    for n in range(len(order) + 2):
        if 0 < n < len(order):
            steps.append(functools.partial(rest_z, *order[n]))
        if 0 <= n - 1 < len(order):
            steps.append(functools.partial(rest_plane, *order[n - 1]))
        if 0 <= n - 2 < len(order):
            steps.append(functools.partial(rest_diag, *order[n - 2]))

    def advance(count):
        for _ in range(min(count, len(steps))):
            steps.pop(0)()

    hid_start()
    wq_start()
    rest_start()

    half = HEAD_DIM // 2
    lane = lax.broadcasted_iota(jnp.int32, (tokens, LANES), 1) % half
    freq = jnp.exp(lane.astype(F32) * (-2.0 / HEAD_DIM * math.log(rope_base)))
    row = lax.broadcasted_iota(jnp.int32, (tokens, LANES), 0).astype(F32)
    cos_ref[...] = jnp.cos(row * freq)
    sin_ref[...] = jnp.sin(row * freq)

    wq_z()
    hid_step(1)
    wq_plane()
    hid_step(2)
    wq_diag()
    for k in range(3, depth):
        hid_step(k)
    advance(2)
    wq_sib()
    for slot_id in range(3):
        ref, dst = ((hidden_ref, hid(t)), (wq_ref.at[z], wq_all.at[mine]), (rest_ref, rest(mine)))[slot_id]
        pltpu.make_async_copy(ref, dst, own_sems.at[slot_id]).wait()
    for zz in range(depth):
        i = 2 * zz + 1 - c
        arrive(hid(i), hid_sems.at[i])

    rows = wq_all.shape[0] * wq_all.shape[1]
    for j in range(3):
        wq_out[:, TYPE * j : TYPE * (j + 1)] = (
            wq_all[:, :, TYPE * j : TYPE * (j + 1)].astype(F32).reshape(rows, TYPE).astype(BF16)
        )
    gain = jnp.transpose(wq_all[:, :, 3 * TYPE :].astype(F32).reshape(rows, LANES))[0:1, :]
    gain_out[...] = gain
    advance(1)

    def turn(x, cos, sin):
        a, d = x[:, :LANES], x[:, LANES:]
        return jnp.concatenate([a * cos - d * sin, d * cos + a * sin], axis=1)

    def project(p, _):
        base_row = lax.broadcasted_iota(jnp.int32, (8, LANES), 0)
        lane8 = lax.broadcasted_iota(jnp.int32, (8, LANES), 1) % half
        freq8 = jnp.exp(lane8.astype(F32) * (-2.0 / HEAD_DIM * math.log(rope_base)))
        parts, coss, sins = [], [], []
        for cc in range(2):
            blk = 2 * p + cc
            x = hid_all[blk].astype(F32)
            centre = jnp.mean(x, axis=-1, keepdims=True)
            x = x - centre
            inv = lax.rsqrt(jnp.mean(x * x, axis=-1, keepdims=True) + norm_eps)
            parts.append((x * inv * gain).astype(BF16))
            start = (blk * tokens + base_row * 0).astype(F32) * freq8
            cs, sn = jnp.cos(start)[0:1], jnp.sin(start)[0:1]
            coss.append(cos_ref[...] * cs - sin_ref[...] * sn)
            sins.append(sin_ref[...] * cs + cos_ref[...] * sn)
        h = jnp.concatenate(parts, axis=0)
        h1_ref[pl.ds(p * 2 * tokens, 2 * tokens), :] = h
        qkv = jnp.dot(h, wq_out[...], preferred_element_type=F32)
        cos, sin = jnp.concatenate(coss, axis=0), jnp.concatenate(sins, axis=0)
        kr = turn(qkv[:, TYPE : 2 * TYPE], cos, sin)
        k_ref[pl.ds(p * 2 * tokens, 2 * tokens), :] = kr.astype(BF16)
        v_ref[pl.ds(p * 2 * tokens, 2 * tokens), :] = qkv[:, 2 * TYPE :].astype(BF16)
        qr = turn(qkv[:, :TYPE], cos, sin).astype(BF16)
        qr = jnp.where(c == 0, qr[:tokens].astype(F32), qr[tokens:].astype(F32))
        q_ref[pl.ds(p * tokens, tokens), :] = (qr * HEAD_DIM**-0.5).astype(BF16)
        return 0

    lax.fori_loop(0, depth, project, 0)
    advance(2)

    lane_id = lax.broadcasted_iota(jnp.int32, (1, TYPE), 1)
    lse_lane = lax.broadcasted_iota(jnp.int32, (1, LANES), 1)

    def attend(p, _):
        at = pl.ds(p * tokens, tokens)
        q = q_ref[at, :].astype(F32)
        out = jnp.zeros((tokens, TYPE), F32)
        lse = jnp.zeros((tokens, LANES), F32)
        for h in range(heads):
            rope_mask = ((lane_id % LANES) // half == h).astype(F32)
            val_mask = (lane_id // HEAD_DIM == h).astype(F32)
            s = lax.dot_general(
                (q * rope_mask).astype(BF16),
                k_ref[...],
                (((1,), (1,)), ((), ())),
                preferred_element_type=F32,
            )
            peak = jnp.max(s, axis=-1, keepdims=True)
            e = jnp.exp(s - peak)
            total = jnp.sum(e, axis=-1, keepdims=True)
            mix = jnp.dot(e.astype(BF16), v_ref[...], preferred_element_type=F32)
            out = out + mix * (val_mask / total)
            lse = lse + (peak + jnp.log(total)) * (lse_lane == h).astype(F32)
        o_ref[at, :] = out.astype(BF16)
        att_own[p] = out.astype(BF16)
        lse_ref[at, :] = lse
        return 0

    for p in range(depth):
        attend(p, 0)
        zz = p
        sends.go(
            att_own.at[p],
            att_ref.at[z],
            att_sems.at[z],
            b,
            2 * zz + c,
            cond=z != p,
        )
        advance(3)
    advance(len(steps))
    att_ref[z] = att_own[z]
    for k in range(1, depth):
        zz = (z + k) % depth
        arrive(att_ref.at[zz], att_sems.at[zz])
    rest_sib()
    sends.drain()


def front(hidden, wq_pack, rest_pack, depth, heads):
    tokens, width = hidden.shape
    shards = 8 * depth
    drows = rest_pack.shape[0]
    whole = pl.BlockSpec(memory_space=pltpu.VMEM)
    hbm = pl.BlockSpec(memory_space=pl.ANY)
    total = 2 * depth * tokens
    out_shape = (
        jax.ShapeDtypeStruct((shards,) + rest_pack.shape, BF16),
        jax.ShapeDtypeStruct((depth, tokens, TYPE), BF16),
        jax.ShapeDtypeStruct((depth * tokens, TYPE), BF16),
        jax.ShapeDtypeStruct((total, TYPE), BF16),
        jax.ShapeDtypeStruct((total, TYPE), BF16),
        jax.ShapeDtypeStruct((depth * tokens, TYPE), BF16),
        jax.ShapeDtypeStruct((depth * tokens, LANES), F32),
        jax.ShapeDtypeStruct((total, width), BF16),
        jax.ShapeDtypeStruct((shards * drows, 3 * TYPE), BF16),
        jax.ShapeDtypeStruct((1, width), F32),
    )
    return pl.pallas_call(
        functools.partial(front_kernel, depth, tokens, heads),
        out_shape=out_shape,
        in_specs=[whole, whole, hbm],
        out_specs=[hbm] + [whole] * 9,
        scratch_shapes=[
            pltpu.VMEM((2 * depth, tokens, width), BF16),
            pltpu.VMEM((shards, drows, 3 * TYPE + LANES), BF16),
            pltpu.VMEM((depth, tokens, TYPE), BF16),
            pltpu.VMEM((tokens, LANES), F32),
            pltpu.VMEM((tokens, LANES), F32),
            pltpu.SemaphoreType.DMA((160,)),
            pltpu.SemaphoreType.DMA((2 * depth,)),
            pltpu.SemaphoreType.DMA((shards,)),
            pltpu.SemaphoreType.DMA((shards,)),
            pltpu.SemaphoreType.DMA((2, shards)),
            pltpu.SemaphoreType.DMA((depth,)),
            pltpu.SemaphoreType.DMA((3,)),
        ],
        compiler_params=pltpu.CompilerParams(
            collective_id=0, has_side_effects=True, vmem_limit_bytes=56 * 2**20
        ),
    )(hidden, wq_pack, rest_pack)


def pack_heads(w_qkv, depth, heads):
    half = HEAD_DIM // 2
    rows = w_qkv.shape[0]
    used = heads * half
    pads = ((0, 0), (0, 0), (0, 0), (0, LANES - used))
    qk = w_qkv[:, : 2 * D].reshape(rows, 2, depth, heads, 2, half)
    qk = jnp.transpose(qk, (2, 0, 1, 4, 3, 5)).reshape(depth, rows, 4, used)
    qk = jnp.pad(qk, pads).reshape(depth, rows, 2 * TYPE)
    v = jnp.transpose(w_qkv[:, 2 * D :].reshape(rows, depth, heads * HEAD_DIM), (1, 0, 2))
    v = jnp.pad(v, ((0, 0), (0, 0), (0, TYPE - heads * HEAD_DIM)))
    return jnp.concatenate([qk, v], axis=2)


def back_kernel(
    depth,
    tokens,
    heads,
    splits,
    datt_ref,
    q_ref,
    k_ref,
    v_ref,
    o_ref,
    lse_ref,
    h1_ref,
    wq_ref,
    lt_ref,
    lt_send,
    rt_ref,
    gain2_ref,
    gain2_send,
    hidden_ref,
    gain_ref,
    dres_ref,
    rest_out,
    qkv_out,
    hid_out,
    gain_out,
    dat_all,
    lt_all,
    rt_all,
    gain2_all,
    grads,
    hx,
    hy,
    fx,
    fy,
    ssum,
    rz,
    dq_acc,
    dk_acc,
    dv_acc,
    part_own,
    part_all,
    dqkv,
    dh_own,
    dh_all,
    qg_wide,
    qg,
    qhx,
    qhy,
    qfx,
    qfy,
    qsum,
    qz,
    gain_row,
    gain_all,
    send_sems,
    dat_sems,
    sib_sems,
    half_sems,
    full_sems,
    z_sems,
    part_sems,
    dh_sems,
    q_sems,
    qz_sems,
    gain_sems,
):
    b, z, c = place()
    t = 2 * z + c
    bx, by = plane_x(b), plane_y(b)
    bd = plane_x(by)
    sib = (b, 2 * z + 1 - c)
    everyone = [
        ((b + i) % 4, (t + j) % (2 * depth)) for i in range(4) for j in range(2 * depth) if i + j
    ]
    greet(everyone)
    sends = Sends(send_sems)
    half = HEAD_DIM // 2

    def arrive(dst, sem):
        remote(dst, dst, send_sems.at[0], sem, *sib).wait_recv()

    def others():
        return [(z + k) % depth for k in range(1, depth)]

    for j, (src, dst) in enumerate(
        ((lt_send, lt_all), (rt_ref, rt_all), (gain2_send, gain2_all))
    ):
        sends.go(src, dst, sib_sems.at[j], *sib)
    for zz in others():
        sends.go(datt_ref.at[zz], dat_all.at[z], dat_sems.at[z], b, 2 * zz + c)
    dat_all[z] = datt_ref[z]

    for j, (dst,) in enumerate(((lt_all,), (rt_all,), (gain2_all,))):
        arrive(dst, sib_sems.at[j])
    rows = lt_ref.shape[1]
    drows = rows // (4 * depth)
    step = math.gcd(*splits)
    col = 0
    for i, part in enumerate(splits):
        left = jnp.concatenate([lt_ref[i], lt_all[i]], axis=1)
        for _ in range(part // step):
            right = jnp.concatenate(
                [rt_ref[:, col : col + step], rt_all[:, col : col + step]], axis=0
            )
            term = jnp.dot(left, right, preferred_element_type=F32)
            grads[:, :, col : col + step] = term.reshape(4 * depth, drows, step).astype(BF16)
            col += step
    grads[:, :, col:] = (gain2_ref[...].astype(F32) + gain2_all[...].astype(F32)).astype(BF16)
    width = grads.shape[2]
    cut = width // 2 // LANES * LANES
    part_a, part_b = pl.ds(0, cut), pl.ds(cut, width - cut)

    def at(bb, zz):
        return bb * depth + zz

    def rest_start():
        for zz in range(depth):
            sends.go(grads.at[at(bd, zz), :, part_a], hx.at[zz], half_sems.at[0, zz], bx, t)
            sends.go(grads.at[at(bd, zz), :, part_b], hy.at[zz], half_sems.at[1, zz], by, t)

    def rest_half(zz):
        arrive(hx.at[zz], half_sems.at[0, zz])
        i = at(by, zz)
        grads[i, :, :cut] = (grads[i, :, :cut].astype(F32) + hx[zz].astype(F32)).astype(BF16)
        sends.go(grads.at[i], fy.at[zz], full_sems.at[1, zz], by, t)
        arrive(hy.at[zz], half_sems.at[1, zz])
        i = at(bx, zz)
        grads[i, :, cut:] = (grads[i, :, cut:].astype(F32) + hy[zz].astype(F32)).astype(BF16)
        sends.go(grads.at[i], fx.at[zz], full_sems.at[0, zz], bx, t)

    def rest_full(zz):
        arrive(fx.at[zz], full_sems.at[0, zz])
        arrive(fy.at[zz], full_sems.at[1, zz])
        total = grads[at(b, zz)].astype(F32) + fx[zz].astype(F32) + fy[zz].astype(F32)

        @pl.when(z == zz)
        def _():
            rest_out[...] = total

        @pl.when(z != zz)
        def _():
            ssum[zz] = total.astype(BF16)

        sends.go(ssum.at[zz], rz.at[z], z_sems.at[z], b, 2 * zz + c, cond=z != zz)

    def rest_final():
        for zz in others():
            arrive(rz.at[zz], z_sems.at[zz])
            rest_out[...] += rz[zz].astype(F32)

    steps = []
    for zz in range(depth + 1):
        if zz < depth:
            steps.append(functools.partial(rest_half, zz))
        if zz > 0:
            steps.append(functools.partial(rest_full, zz - 1))

    def advance(count):
        for _ in range(min(count, len(steps))):
            steps.pop(0)()

    rest_start()
    for zz in others():
        arrive(dat_all.at[zz], dat_sems.at[zz])

    lane_id = lax.broadcasted_iota(jnp.int32, (1, TYPE), 1)
    lse_lane = lax.broadcasted_iota(jnp.int32, (1, LANES), 1)
    rope_masks = [((lane_id % LANES) // half == h).astype(F32) for h in range(heads)]
    val_masks = [(lane_id // HEAD_DIM == h).astype(F32) for h in range(heads)]
    last = (((1,), (1,)), ((), ()))
    first = (((0,), (0,)), ((), ()))

    def attend(p):
        rows_p = slice(p * tokens, (p + 1) * tokens)
        q = q_ref[rows_p, :].astype(F32)
        da = dat_all[p].astype(F32)
        mixed = da * o_ref[rows_p, :].astype(F32)
        lse = lse_ref[rows_p, :]
        qs = jnp.concatenate([(q * m).astype(BF16) for m in rope_masks], axis=0)
        das = jnp.concatenate([(da * m).astype(BF16) for m in val_masks], axis=0)
        delta = jnp.concatenate(
            [jnp.sum(mixed * m, axis=-1, keepdims=True) for m in val_masks], axis=0
        )
        lses = jnp.concatenate(
            [
                jnp.sum(lse * (lse_lane == h).astype(F32), axis=-1, keepdims=True)
                for h in range(heads)
            ],
            axis=0,
        )
        s = lax.dot_general(qs, k_ref[...], last, preferred_element_type=F32)
        prob = jnp.exp(s - lses)
        dp = lax.dot_general(das, v_ref[...], last, preferred_element_type=F32)
        ds = (prob * (dp - delta)).astype(BF16)
        low = prob.astype(BF16)
        dq = jnp.dot(ds, k_ref[...], preferred_element_type=F32)
        total = dq[:tokens] * rope_masks[0]
        for h in range(1, heads):
            total = total + dq[h * tokens : (h + 1) * tokens] * rope_masks[h]
        dq_acc[rows_p, :] = total * HEAD_DIM**-0.5
        dk = lax.dot_general(ds, qs, first, preferred_element_type=F32)
        dv = lax.dot_general(low, das, first, preferred_element_type=F32)
        if p == 0:
            dk_acc[...] = dk
            dv_acc[...] = dv
        else:
            dk_acc[...] += dk
            dv_acc[...] += dv

    for p in range(depth):
        attend(p)
        advance(2)

    row = lax.broadcasted_iota(jnp.int32, (tokens, LANES), 0)
    lane = lax.broadcasted_iota(jnp.int32, (tokens, LANES), 1) % half
    freq = jnp.exp(lane.astype(F32) * (-2.0 / HEAD_DIM * math.log(rope_base)))
    base_cos, base_sin = jnp.cos(row.astype(F32) * freq), jnp.sin(row.astype(F32) * freq)

    def unturn(x, blk):
        start = (blk * tokens + row[:8] * 0).astype(F32) * freq[:8]
        cs, sn = jnp.cos(start)[0:1], jnp.sin(start)[0:1]
        cos = base_cos * cs - base_sin * sn
        sin = base_sin * cs + base_cos * sn
        a, d = x[:, :LANES], x[:, LANES:]
        return jnp.concatenate([a * cos + d * sin, d * cos - a * sin], axis=1)

    for blk in range(2 * depth):
        span = slice(blk * tokens, (blk + 1) * tokens)
        dk_acc[span, :] = unturn(dk_acc[span, :], blk)
    part_own[: 2 * depth * tokens, :TYPE] = dk_acc[...].astype(BF16)
    part_own[: 2 * depth * tokens, TYPE:] = dv_acc[...].astype(BF16)
    for p in range(depth):
        span = slice(p * tokens, (p + 1) * tokens)
        dq_acc[span, :] = unturn(dq_acc[span, :], 2 * p + c)
    part_q = slice(2 * depth * tokens, 3 * depth * tokens)
    part_own[part_q, :TYPE] = dq_acc[...].astype(BF16)
    sends.go(part_own, part_all, part_sems.at[0], *sib)
    advance(1)
    arrive(part_all, part_sems.at[0])
    whole = 2 * depth * tokens
    dqkv[:, TYPE : 2 * TYPE] = (dk_acc[...] + part_all[:whole, :TYPE].astype(F32)).astype(BF16)
    dqkv[:, 2 * TYPE :] = (dv_acc[...] + part_all[:whole, TYPE:].astype(F32)).astype(BF16)
    for p in range(depth):
        src = slice(whole + p * tokens, whole + (p + 1) * tokens)
        here = part_own[src, :TYPE].astype(F32)
        there = part_all[src, :TYPE].astype(F32)
        even = jnp.where(c == 0, here, there).astype(BF16)
        odd = jnp.where(c == 0, there, here).astype(BF16)
        dqkv[2 * p * tokens : (2 * p + 1) * tokens, :TYPE] = even
        dqkv[(2 * p + 1) * tokens : (2 * p + 2) * tokens, :TYPE] = odd

    for p in range(depth):
        blk = pl.ds((2 * p + c) * tokens, tokens)
        dh = lax.dot_general(dqkv[blk, :], wq_ref[...], last, preferred_element_type=F32)
        dh_own[p] = dh.astype(BF16)
        sends.go(dh_own.at[p], dh_all.at[z], dh_sems.at[z], b, 2 * p + c, cond=z != p)

    for j in range(3):
        cols = slice(TYPE * j, TYPE * (j + 1))
        term = lax.dot_general(h1_ref[...], dqkv[:, cols], first, preferred_element_type=F32)
        qg_wide[...] = term.reshape(4 * depth, 2, drows, TYPE)
        qg[:, :, cols] = qg_wide[:, c].astype(BF16)
    low_z, high_z = pl.ds(0, depth // 2), pl.ds(depth // 2, depth - depth // 2)

    def qrows(bb):
        return pl.ds(bb * depth, depth)

    def qlow(bb):
        return pl.ds(bb * depth, depth // 2)

    def qhigh(bb):
        return pl.ds(bb * depth + depth // 2, depth - depth // 2)

    sends.go(qg.at[qlow(bd)], qhx, q_sems.at[0], bx, t)
    sends.go(qg.at[qhigh(bd)], qhy, q_sems.at[1], by, t)
    advance(len(steps))
    arrive(qhx, q_sems.at[0])
    qg[qlow(by)] = (qg[qlow(by)].astype(F32) + qhx[...].astype(F32)).astype(BF16)
    sends.go(qg.at[qrows(by)], qfy, q_sems.at[3], by, t)
    arrive(qhy, q_sems.at[1])
    qg[qhigh(bx)] = (qg[qhigh(bx)].astype(F32) + qhy[...].astype(F32)).astype(BF16)
    sends.go(qg.at[qrows(bx)], qfx, q_sems.at[2], bx, t)

    grad = dh_own[z].astype(F32)
    for zz in others():
        arrive(dh_all.at[zz], dh_sems.at[zz])
        grad = grad + dh_all[zz].astype(F32)
    x = hidden_ref[...].astype(F32)
    centre = jnp.mean(x, axis=-1, keepdims=True)
    x = x - centre
    inv = lax.rsqrt(jnp.mean(x * x, axis=-1, keepdims=True) + norm_eps)
    x = x * inv
    gain_row[...] = jnp.sum(grad * x, axis=0, keepdims=True)
    me = b * 2 * depth + t
    for bb, tt in everyone:
        sends.go(gain_row, gain_all.at[me], gain_sems.at[me], bb, tt)
    e = grad * gain_ref[...]
    hid_out[...] = dres_ref[...] + inv * (
        e - jnp.mean(e, axis=-1, keepdims=True) - x * jnp.mean(e * x, axis=-1, keepdims=True)
    )

    arrive(qfx, q_sems.at[2])
    arrive(qfy, q_sems.at[3])
    total = qg[qrows(b)].astype(F32) + qfx[...].astype(F32) + qfy[...].astype(F32)
    qsum[...] = total.astype(BF16)
    for zz in others():
        sends.go(qsum.at[zz], qz.at[z], qz_sems.at[z], b, 2 * zz + c)
    qkv_out[z] = qsum[z].astype(F32)
    rest_final()
    for zz in others():
        arrive(qz.at[zz], qz_sems.at[zz])
        qkv_out[zz] = qz[zz].astype(F32)
    gains = gain_row[...]
    for bb, tt in everyone:
        i = bb * 2 * depth + tt
        arrive(gain_all.at[i], gain_sems.at[i])
        gains = gains + gain_all[i]
    gain_out[...] = gains
    sends.drain()


def back(depth, heads, splits, *operands):
    tokens, width = operands[13].shape
    drows = operands[8].shape[1] // (4 * depth)
    cols = sum(splits) + LANES
    cut = cols // 2 // LANES * LANES
    total = 2 * depth * tokens
    vm = pltpu.VMEM
    dma = pltpu.SemaphoreType.DMA
    whole = pl.BlockSpec(memory_space=pltpu.VMEM)
    blocks = 4 * depth
    return pl.pallas_call(
        functools.partial(back_kernel, depth, tokens, heads, splits),
        out_shape=(
            jax.ShapeDtypeStruct((drows, cols), F32),
            jax.ShapeDtypeStruct((depth, drows, 3 * TYPE), F32),
            jax.ShapeDtypeStruct((tokens, width), F32),
            jax.ShapeDtypeStruct((1, width), F32),
        ),
        in_specs=[whole] * len(operands),
        out_specs=[whole] * 4,
        scratch_shapes=[
            vm((depth, tokens, TYPE), BF16),
            vm(operands[8].shape, BF16),
            vm(operands[10].shape, BF16),
            vm(operands[11].shape, BF16),
            vm((blocks, drows, cols), BF16),
            vm((depth, drows, cut), BF16),
            vm((depth, drows, cols - cut), BF16),
            vm((depth, drows, cols), BF16),
            vm((depth, drows, cols), BF16),
            vm((depth, drows, cols), BF16),
            vm((depth, drows, cols), BF16),
            vm((depth * tokens, TYPE), F32),
            vm((total, TYPE), F32),
            vm((total, TYPE), F32),
            vm((3 * depth * tokens, 2 * TYPE), BF16),
            vm((3 * depth * tokens, 2 * TYPE), BF16),
            vm((total, 3 * TYPE), BF16),
            vm((depth, tokens, width), BF16),
            vm((depth, tokens, width), BF16),
            vm((blocks, 2, drows, TYPE), F32),
            vm((blocks, drows, 3 * TYPE), BF16),
            vm((depth // 2, drows, 3 * TYPE), BF16),
            vm((depth - depth // 2, drows, 3 * TYPE), BF16),
            vm((depth, drows, 3 * TYPE), BF16),
            vm((depth, drows, 3 * TYPE), BF16),
            vm((depth, drows, 3 * TYPE), BF16),
            vm((depth, drows, 3 * TYPE), BF16),
            vm((1, width), F32),
            vm((8 * depth, 1, width), F32),
            dma((96,)),
            dma((depth,)),
            dma((3,)),
            dma((2, depth)),
            dma((2, depth)),
            dma((depth,)),
            dma((1,)),
            dma((depth,)),
            dma((4,)),
            dma((depth,)),
            dma((8 * depth,)),
        ],
        compiler_params=pltpu.CompilerParams(
            collective_id=1, has_side_effects=True, vmem_limit_bytes=60 * 2**20
        ),
    )(*operands)


def unpack_heads(grad, depth, heads):
    half = HEAD_DIM // 2
    rows = grad.shape[1]
    qk = grad[:, :, : 2 * TYPE].reshape(depth, rows, 2, 2, LANES)[..., : heads * half]
    qk = qk.reshape(depth, rows, 2, 2, heads, half)
    qk = jnp.transpose(qk, (1, 2, 0, 4, 3, 5)).reshape(rows, 2 * D)
    v = jnp.transpose(grad[:, :, 2 * TYPE : 2 * TYPE + heads * HEAD_DIM], (1, 0, 2))
    return jnp.concatenate([qk, v.reshape(rows, D)], axis=1)


def by_heads(
    depth, heads, hidden, cotangent, w_qkv, w_proj, w_inner, w_down, norm1_gain, norm2_gain
):
    tokens = hidden.shape[1]
    rows = w_qkv.shape[0]
    core = lax.axis_index("ctx") % 2
    column = lambda gain: jnp.pad(gain[:, None], ((0, 0), (0, LANES - 1)))
    gain_block = jnp.broadcast_to(column(norm1_gain)[None], (depth, rows, LANES))
    wq_pack = jnp.concatenate([pack_heads(w_qkv, depth, heads), gain_block], axis=2)
    rest_pack = jnp.concatenate([w_proj, w_inner, w_down, column(norm2_gain)], axis=1)
    rest_all, att, q, k, v, o, lse, h1, wq, first_gain = front(
        hidden[0], wq_pack, rest_pack, depth, heads
    )
    rest_all = rest_all.reshape(D, rest_pack.shape[1])
    splits = (w_proj.shape[1], w_inner.shape[1], w_down.shape[1])
    edges = [0]
    for part in splits:
        edges.append(edges[-1] + part)
    full_proj, full_inner, full_down = (rest_all[:, edges[i] : edges[i + 1]] for i in range(3))
    second_norm_gain = rest_all[:, edges[3]].astype(F32)
    used = heads * HEAD_DIM
    attended = jnp.transpose(att[:, :, :used], (1, 0, 2)).reshape(tokens, D)
    residual_stream = hidden[0].astype(F32) + jnp.dot(
        attended, full_proj, preferred_element_type=F32
    )
    second_normed_rows, second_centered_rows, second_inverse_deviation = apply_layer_norm(
        residual_stream, second_norm_gain
    )
    h_two = second_normed_rows.astype(BF16)
    inner_all = jnp.dot(h_two, full_inner, preferred_element_type=F32)
    act_half = inner_all[:, :FF]
    gate_half = inner_all[:, FF:]
    activated, gelu_slope = gelu_parts(act_half)
    middle = (activated * gate_half).astype(BF16)
    output_rows = residual_stream + jnp.einsum(
        "tf,df->td", middle, full_down, preferred_element_type=F32
    )
    upstream = cotangent[0]
    d_middle = jnp.dot(upstream, full_down, preferred_element_type=F32)
    d_inner = jnp.concatenate(
        [d_middle * gate_half * gelu_slope, d_middle * activated], axis=-1
    ).astype(BF16)
    second_hidden_gradient = jnp.einsum(
        "te,de->td", d_inner, full_inner, preferred_element_type=F32
    )
    residual_norm_gradient, second_gain_portion = layer_norm_gradient(
        second_hidden_gradient, second_norm_gain, second_centered_rows, second_inverse_deviation
    )
    d_resid = upstream.astype(F32) + residual_norm_gradient
    d_resid_low = d_resid.astype(BF16)
    d_attended = jnp.einsum(
        "td,ed->te", d_resid_low, full_proj, preferred_element_type=F32
    ).astype(BF16)
    datt = jnp.pad(
        jnp.transpose(d_attended.reshape(tokens, depth, used), (1, 0, 2)),
        ((0, 0), (0, 0), (0, TYPE - used)),
    )
    lefts = jnp.stack([jnp.transpose(a) for a in (attended, h_two, upstream)])
    lefts = lefts.reshape(3, 4 * depth, 2, rows, tokens)
    gains = jnp.pad(second_gain_portion[:, None], ((0, 0), (0, LANES - 1))).astype(BF16)
    gains = gains.reshape(4 * depth, 2, rows, LANES)

    def lane_of(array, axis, which):
        return lax.dynamic_index_in_dim(array, which, axis, keepdims=False)

    def left_of(which):
        return lane_of(lefts, 2, which).reshape(3, 4 * depth * rows, tokens)

    rights = jnp.concatenate([d_resid_low, d_inner, middle], axis=1)
    rest_grad, qkv_grad, hidden_grad, gain_total = back(
        depth,
        heads,
        splits,
        datt,
        q,
        k,
        v,
        o,
        lse,
        h1,
        wq,
        left_of(core),
        left_of(1 - core),
        rights,
        lane_of(gains, 1, core),
        lane_of(gains, 1, 1 - core),
        hidden[0],
        first_gain,
        d_resid,
    )
    own = (lax.axis_index("batch") * 2 * depth + lax.axis_index("ctx")) * rows
    return (
        output_rows.astype(BF16)[None],
        hidden_grad[None],
        unpack_heads(qkv_grad, depth, heads),
        rest_grad[:, edges[0] : edges[1]],
        rest_grad[:, edges[1] : edges[2]],
        rest_grad[:, edges[2] : edges[3]],
        lax.dynamic_slice_in_dim(gain_total[0], own, rows),
        rest_grad[:, edges[3]],
    )


def solution(mesh):
    placed = (
        P("batch", "ctx", None),
        P("batch", "ctx", None),
        P(("batch", "ctx"), None),
        P(("batch", "ctx"), None),
        P(("batch", "ctx"), None),
        P(("batch", "ctx"), None),
        P(("batch", "ctx")),
        P(("batch", "ctx")),
    )
    width = mesh.shape["ctx"]
    depth = width // 2
    heads = HEADS // max(depth, 1)
    plane = mesh.shape["batch"] == 4 and width == 2 * depth and depth % 2 == 0
    fits = heads * depth == HEADS and heads * HEAD_DIM <= TYPE and heads * HEAD_DIM <= 2 * LANES
    body = functools.partial(by_heads, depth, heads) if plane and fits else local
    return jax.shard_map(
        body,
        mesh=mesh,
        in_specs=placed,
        out_specs=(
            P("batch", "ctx", None),
            P("batch", "ctx", None),
            P(("batch", "ctx"), None),
            P(("batch", "ctx"), None),
            P(("batch", "ctx"), None),
            P(("batch", "ctx"), None),
            P(("batch", "ctx")),
            P(("batch", "ctx")),
        ),
        check_vma=False,
    )
```
